32 devices in a mesh: tile: 4 (over z), chan: 4 (over y, x), tm: 2 (over core).
Axes of the slice: x: 2, y: 2, z: 4, core: 2. Of those that a mesh axis runs over, the one named last changes fastest.
Arguments:
- observed_values: bfloat16 [2, 65536, 128], P('tm', ('tile', 'chan')), may hold values from -6 to 6
- observed_tile: int32 [2, 65536, 1], P('tm', ('tile', 'chan')), may hold values from 0 to 3; in each aligned block of 4096 rows (0 to 4095, 4096 to 8191, ..., all dimensions but the last counted through in order) at most 2048 rows name the same one
- observed_cell: int32 [2, 65536], P('tm', ('tile', 'chan')), may hold values from 0 to 2047
- patch_weight: bfloat16 [4, 256, 256], P(None, None, 'chan'), may hold values from -0.1875 to 0.1875
- depth_weight: bfloat16 [9, 256], P(None, 'chan'), may hold values from -2 to 2
- owners: int32 [4, 4], replicated, may hold values from 0 to 3, as said below
Outputs:
- owned: bfloat16 [4, 2, 4, 64, 256], P('tile', 'tm', None, None, 'chan')
The draws below stay inside these ranges and needn't reach their ends.
Inputs may be any that keep to these rules, and one draw needn't show every extreme that they name: `observed_tile`: in the rows of one device at most 2048 name the same tile. owners[t, j] - t is the same modulo 4 for every t and differs between any two j, so every row and every column of owners is a permutation.
All inputs are finite; a program needn't handle non-finite values.
Results may differ from the reference program's by a relative error of at most 0.014.
Values may be sent and summed in bfloat16 or wider, within the bound.
A program may use at most 64 MiB of HBM per device.

```python
import math
import jax
import jax.numpy as jnp
import numpy as np

V = 128
LAT = 256
HS = 32
WS = 64
OBS_DEV = 4096
CELLS = 2048
CAP = 2048
OBS_ALL = 65536
CHANNELS = 256
HR = 8
PC = 64
N_TILE = 4
N_TM = 2


def draw_owners(key, part):
    shifts = jax.random.permutation(jax.random.fold_in(key, 17), N_TILE)
    sources = jnp.arange(N_TILE)[:, None]
    return ((sources + shifts[None, :]) % N_TILE).astype(jnp.int32)


def with_ends(entries, key, smallest, largest):
    longest = entries.shape.index(max(entries.shape))
    spots = []
    for shift in (0, 1):
        where = [jax.random.randint(jax.random.fold_in(key, axis), (), 0, length) for axis, length in enumerate(entries.shape)]
        where[longest] = (where[longest] + shift) % entries.shape[longest]
        spots.append(tuple(where))
    return entries.at[spots[0]].set(smallest).at[spots[1]].set(largest)


def steps_of(rng, extent, split, least, top_value):
    loudness = 1.0
    for dim, blocks in split:
        heights = jax.random.uniform(jax.random.fold_in(jax.random.fold_in(rng, 6), dim), (blocks,), jnp.float32, least / len(split), top_value / len(split))
        loudness = loudness * jnp.repeat(jnp.exp(heights), extent[dim] // blocks).reshape((-1,) + (1,) * (len(extent) - 1 - dim))
    return loudness


def routed_block(rng, own, number, rows, amount, top, bound, skew):
    order = jax.random.permutation(rng, amount)
    packed, usual = shares(amount, rows * top, bound, skew, True), shares(amount, rows * top, bound, skew, False)
    places = jnp.arange(amount)

    def named(tallies, rotation):
        used = int((tallies > 0).sum())
        fixed = max(1, used // 4)
        moved = fixed + (places - fixed + rotation * (used - fixed)) % max(1, amount - fixed)
        return jnp.zeros((amount,), jnp.int32).at[order[jnp.where(places < fixed, places, moved)]].set(jnp.asarray(tallies, jnp.int32))

    tallies = jnp.where(number % 4 == 0, named(packed, number // 4), named(usual, number - number // 4 - 1))
    mixed = jax.random.permutation(jax.random.fold_in(own, 3), amount)
    source_of, receiver = mixed[0:amount // 2 * 2:2], mixed[1:amount // 2 * 2:2]
    slack = jnp.minimum(tallies[source_of] - 1, bound - tallies[receiver]) // 2
    slack = jnp.where((source_of == order[0]) | (receiver == order[0]) | (tallies[receiver] == 0), 0, jnp.maximum(slack, 0))
    moved = jax.random.randint(jax.random.fold_in(own, 4), (amount // 2,), 0, 1 << 20) % (slack + 1)
    tallies = tallies.at[source_of].add(-moved).at[receiver].add(moved)
    labels = jnp.searchsorted(jnp.cumsum(tallies), jnp.arange(rows * top), side="right").astype(jnp.int32)
    table = labels.reshape(top, rows).T
    table = table[jax.random.permutation(jax.random.fold_in(own, 1), rows)]
    rotation = jax.random.randint(jax.random.fold_in(own, 2), (rows, 1), 0, top)
    return jnp.take_along_axis(table, (jnp.arange(top)[None, :] + rotation) % top, axis=1)


def shares(count, total, bound, lean, full):
    portions = [(1 << 20) // math.isqrt(rank ** lean) + 1 for rank in range(1, count + 1)]
    largest = bound if full else min(bound, max(-(-total // count), total * portions[0] // sum(portions)))
    least = 1 if total - largest >= count - 1 else 0
    given, spare = [largest] + [least] * (count - 1), total - largest - least * (count - 1)
    while spare > 0:
        movable = [i for i in range(1, count) if given[i] < largest] or [i for i in range(1, count) if given[i] < bound]
        pool, remaining = sum([portions[i] for i in movable]), spare
        for i in movable:
            more = min(bound - given[i], max(1, remaining * portions[i] // pool), spare)
            given[i] = given[i] + more
            spare = spare - more
    return np.array(given)


def normal_values(own_key, extent, deviation, most, cuts=(), dtype=jnp.bfloat16):
    values = deviation * jax.random.normal(own_key, extent, jnp.float32)
    if cuts:
        values = values * steps_of(own_key, extent, cuts, -0.22, 0.18)
    return jnp.clip(values, -most, most).astype(dtype)


def setup_inputs(seed: int = 0) -> dict:
    splits = jax.random.split(jax.random.key(seed), 7)
    observed_values = normal_values(splits[0], (N_TM, OBS_ALL, V), 1.0, 6.0, ((0, 2), (1, 16)))
    observed_tile_keys = jax.random.split(jax.random.fold_in(splits[1], 1), N_TM * OBS_ALL // OBS_DEV)
    observed_tile_turns = jax.random.permutation(jax.random.fold_in(splits[1], 3), N_TM * OBS_ALL // OBS_DEV)
    observed_tile = jax.vmap(lambda own, number: routed_block(jax.random.fold_in(splits[1], 2), own, number, OBS_DEV, N_TILE, 1, CAP, 2))(observed_tile_keys, observed_tile_turns).reshape((N_TM, OBS_ALL, 1))
    observed_cell = with_ends(jax.random.randint(splits[2], (N_TM, OBS_ALL), 0, CELLS), jax.random.fold_in(splits[2], 1), 0, CELLS - 1).astype(jnp.int32)
    patch_weight = normal_values(splits[3], (4, CHANNELS, LAT), (4 * CHANNELS) ** -0.5, 0.1875, ((2, 4),))
    depth_weight = normal_values(splits[4], (9, LAT), 9 ** -0.5, 2.0, ((1, 4),))
    owners = draw_owners(jax.random.fold_in(splits[6], 71), 0)
    return dict(observed_values=observed_values, observed_tile=observed_tile, observed_cell=observed_cell, patch_weight=patch_weight, depth_weight=depth_weight, owners=owners)


def reference(observed_values, observed_tile, observed_cell, patch_weight, depth_weight, owners):
    height = HS * N_TILE
    half_cols = WS // 2
    fields = []
    for slot in range(N_TM):
        target = (observed_tile[slot, :, 0] * CELLS + observed_cell[slot]).astype(jnp.int32)
        totals = jax.ops.segment_sum(observed_values[slot].astype(jnp.float32), target, num_segments=N_TILE * CELLS)
        counts = jax.ops.segment_sum(jnp.ones(target.shape, jnp.float32), target, num_segments=N_TILE * CELLS)
        means = (totals / jnp.maximum(counts, 1.0)[:, None]).astype(jnp.bfloat16)
        fields.append(means.reshape(height, WS, V))
    stacked = jnp.concatenate(fields, axis=2)
    encoded = jnp.zeros(((height // 2) * half_cols, LAT), jnp.float32)
    for tap_row in range(2):
        for tap_col in range(2):
            window = stacked[tap_row::2, tap_col::2, :].reshape(-1, CHANNELS)
            encoded = encoded + jnp.dot(window, patch_weight[tap_row * 2 + tap_col], preferred_element_type=jnp.float32)
    hidden = jax.nn.gelu(encoded).astype(jnp.bfloat16).reshape(height // 2, half_cols, LAT)
    widened = jnp.pad(hidden.astype(jnp.float32), ((2, 2), (2, 2), (0, 0)))
    depth = jnp.zeros((height // 2, half_cols, LAT), jnp.float32)
    for tap_row in range(3):
        for tap_col in range(3):
            shifted = widened[2 * tap_row:2 * tap_row + height // 2, 2 * tap_col:2 * tap_col + half_cols, :]
            depth = depth + shifted * depth_weight[tap_row * 3 + tap_col].astype(jnp.float32)
    latent = (hidden.astype(jnp.float32) + depth).astype(jnp.bfloat16)
    pieces = latent.reshape(N_TILE, N_TM, HR, half_cols, LAT).reshape(N_TILE, N_TM, N_TILE, PC, LAT)
    order = jnp.arange(N_TILE).astype(jnp.int32)
    chosen = jnp.sum(order[None, None, :] * (owners[:, None, :] == order[None, :, None]).astype(jnp.int32), axis=2).astype(jnp.int32)
    gathered = pieces[order[None, :], :, chosen.T]
    return jnp.transpose(gathered, (0, 2, 1, 3, 4))
```

```python
import functools
import jax
import jax.numpy as jnp
from jax import lax
from jax.experimental import pallas as pl
from jax.experimental.pallas import tpu as pltpu
from jax.sharding import PartitionSpec as P

V = 128
HS = 32
WS = 64


def padded(x, sides, width):
    for axis, dim in sides:
        devices, length = (lax.axis_size(axis), x.shape[dim])
        up = [(i, (i + 1) % devices) for i in range(devices - 1)]
        down = [(j, i) for i, j in up]
        last = lax.slice_in_dim(x, length - width, length, axis=dim)
        first = lax.slice_in_dim(x, 0, width, axis=dim)
        before = lax.ppermute(last, axis, up)
        after = lax.ppermute(first, axis, down)
        x = jnp.concatenate([before, x, after], axis=dim)
    return x


def pack_rows(values, destination, placed, tile_count, capacity):
    match = (destination[:, None] == lax.iota(jnp.int32, tile_count)[None, :]).astype(jnp.int32)
    earlier = jnp.cumsum(match, axis=0) - match
    position = jnp.sum(earlier * match, axis=1)
    slot_index = destination * capacity + position
    width = values.shape[1]
    sent_values = jnp.zeros((tile_count * capacity, width), jnp.bfloat16).at[slot_index].set(values)
    sent_cells = jnp.full((tile_count * capacity,), -1, jnp.int32).at[slot_index].set(placed)
    return (
        sent_values.reshape(tile_count, capacity, width),
        sent_cells.reshape(tile_count, capacity),
    )


def grid_block(arrived_values, arrived_cells, first_cell):
    cell_ids = first_cell + lax.iota(jnp.int32, 128)
    matches = cell_ids[:, None] == arrived_cells[None, :]
    totals = jnp.dot(
        matches.astype(jnp.bfloat16), arrived_values, preferred_element_type=jnp.float32
    )
    counts = jnp.sum(matches.astype(jnp.float32), axis=1)
    return (totals, counts)


def patch_rows(field, weight, row_start, row_count):
    slab = lax.dynamic_slice_in_dim(field, 2 * row_start, 2 * row_count, 0)
    depth_in = field.shape[2]
    result = jnp.zeros((row_count * (field.shape[1] // 2), weight.shape[2]), jnp.float32)
    for tap_row in range(2):
        for tap_col in range(2):
            window = slab[tap_row::2, tap_col::2, :].reshape(-1, depth_in)
            result = result + jnp.dot(
                window, weight[tap_row * 2 + tap_col], preferred_element_type=jnp.float32
            )
    return result.reshape(row_count, field.shape[1] // 2, weight.shape[2])


def local(observed_values, observed_tile, observed_cell, patch_weight, depth_weight, owners):
    tile_count = lax.axis_size("tile")
    slot_count = lax.axis_size("tm")
    values = observed_values[0]
    capacity = 2 * values.shape[0] // tile_count
    sent_values, sent_cells = pack_rows(
        values, observed_tile[0, :, 0], observed_cell[0], tile_count, capacity
    )
    arrived = (
        lax.all_to_all(sent_values, "tile", split_axis=0, concat_axis=0, tiled=True),
        lax.all_to_all(sent_cells, "tile", split_axis=0, concat_axis=0, tiled=True),
    )
    arrived_values = arrived[0].reshape(-1, V)
    arrived_cells = arrived[1].reshape(-1)
    cell_count = HS * WS
    firsts = jnp.arange(cell_count // 128, dtype=jnp.int32) * 128
    totals, counts = lax.map(
        lambda first_cell: grid_block(arrived_values, arrived_cells, first_cell), firsts
    )
    totals = totals.reshape(cell_count, V)
    counts = counts.reshape(cell_count)
    totals, counts = (
        lax.psum(totals.astype(jnp.bfloat16), "chan").astype(jnp.float32),
        lax.psum(counts.astype(jnp.bfloat16), "chan").astype(jnp.float32),
    )
    means = (totals / jnp.maximum(counts, 1.0)[:, None]).astype(jnp.bfloat16)
    means = means.reshape(HS, WS, V)
    out_rows = HS // (2 * slot_count)
    half_cols = WS // 2
    stacked = lax.all_gather(means, "tm", axis=2, tiled=True)
    encoded = patch_rows(stacked, patch_weight, lax.axis_index("tm") * out_rows, out_rows)
    hidden = jax.nn.gelu(encoded).astype(jnp.bfloat16)
    rimmed = padded(hidden, ((("tile", "tm"), 0),), 2)
    widened = jnp.pad(rimmed, ((0, 0), (2, 2), (0, 0))).astype(jnp.float32)
    depth = jnp.zeros(hidden.shape, jnp.float32)
    for tap_row in range(3):
        for tap_col in range(3):
            shifted = widened[
                2 * tap_row : 2 * tap_row + out_rows, 2 * tap_col : 2 * tap_col + half_cols, :
            ]
            depth = depth + shifted * depth_weight[tap_row * 3 + tap_col].astype(jnp.float32)
    latent = (hidden.astype(jnp.float32) + depth).astype(jnp.bfloat16)
    channels = latent.shape[2]
    pieces = latent.reshape(tile_count, -1, channels)
    own_row = lax.dynamic_index_in_dim(owners, lax.axis_index("tile"), 0, keepdims=False)
    order = lax.iota(jnp.int32, tile_count)
    chosen = jnp.sum(
        order[None, :] * (own_row[None, :] == order[:, None]).astype(jnp.int32), axis=1
    )
    outgoing = pieces[chosen]
    received = lax.all_to_all(outgoing, "tile", split_axis=0, concat_axis=0, tiled=True)
    return received.reshape(1, 1, tile_count, -1, channels)


def fused_kernel(
    values_ref, tile_ref, cell_ref, weight_ref, depth_ref, owners_ref, out_ref,
    masked, onehot, position, partial, first, second_src, second, third_src, third,
    count_src, count_in, weights, mean_src, mean_in, means, hidden_src, hidden_all,
    weight_send, weight_recv, pass_send, pass_recv, count_send, count_recv,
    first_send, first_recv, second_send, second_recv, third_send, third_recv,
    mean_send, mean_recv, hidden_send, hidden_recv,
):
    f32, bf16 = jnp.float32, jnp.bfloat16
    n_tile, n_chan, n_core = (lax.axis_size(a) for a in ("tile", "chan", "tm"))
    me_t, me_c, me_s = (lax.axis_index(a) for a in ("tile", "chan", "tm"))
    rows, width = values_ref.shape
    block = partial.shape[3]
    quarter = block // 4
    flip_x = me_c + 1 - 2 * (me_c % 2)
    flip_y = (me_c + 2) % 4
    diagonal = 3 - me_c
    near = (flip_x, flip_y)
    far = (flip_y, flip_x)
    other = 1 - me_s

    def remote(source, target, send, recv, device):
        return pltpu.make_async_remote_copy(
            src_ref=source, dst_ref=target, send_sem=send, recv_sem=recv,
            device_id=device, device_id_type=pl.DeviceIdType.MESH,
        )

    offsets = [
        (a, b, c) for a in range(n_tile) for b in range(n_chan) for c in range(n_core)
    ][1:]

    def at(a, b, c):
        return ((me_t + a) % n_tile, (me_c + b) % n_chan, (me_s + c) % n_core)

    barrier = pltpu.get_barrier_semaphore()
    for offset in offsets:
        pl.semaphore_signal(
            barrier, inc=1, device_id=at(*offset), device_id_type=pl.DeviceIdType.MESH
        )

    cell = cell_ref[...]
    row, col = cell // WS, cell % WS
    half_cols = WS // 2
    band = row // 4
    position[...] = (
        band * block + (row % 2) * (2 * quarter) + (col % 2) * quarter
        + ((row % 4) // 2) * half_cols + col // 2
    )
    weights[me_c] = weight_ref[...]

    def mask_rows(i, carry):
        span = pl.ds(pl.multiple_of(i * 128, 128), 128)
        tiles = jnp.broadcast_to(tile_ref[:, span].astype(f32), (128, 128))
        tiles = jnp.transpose(tiles)
        taken = values_ref[span, :].astype(f32)
        for t in range(n_tile):
            masked[span, t * width:(t + 1) * width] = jnp.where(
                tiles == float(t), taken, 0.0
            ).astype(bf16)
        return carry

    lax.fori_loop(0, rows // 128, mask_rows, 0)

    pos = position[...]
    inner = pos % block
    half = pos // (block * n_chan)
    piece = (pos // block) % n_chan
    code = ((tile_ref[...] * n_chan + piece) * 8 + half * 2 + inner // 128)
    code_ids = lax.broadcasted_iota(jnp.int32, (n_tile * n_chan * 8, rows), 0)
    lane_ids = lax.broadcasted_iota(jnp.int32, (128, rows), 0)
    counts = lax.dot_general(
        (code_ids == code).astype(bf16), (lane_ids == inner % 128).astype(bf16),
        (((1,), (1,)), ((), ())), preferred_element_type=f32,
    )
    count_src[...] = counts.reshape(n_tile * n_chan, 8, 128)

    pl.semaphore_wait(barrier, len(offsets))

    def weight_copy(o):
        here = weights.at[me_c, me_s]
        return remote(
            here, here, weight_send.at[o - 1], weight_recv.at[o - 1],
            (me_t, (me_c + o) % n_chan, me_s),
        )

    def pass_copy(o):
        here = weights.at[(me_c - o + n_chan) % n_chan, me_s]
        return remote(
            here, here, pass_send.at[o - 1], pass_recv.at[o - 1], (me_t, me_c, other)
        )

    def count_copy(a, b):
        i = a * n_chan + b
        to = ((me_t + a) % n_tile, (me_c + b) % n_chan, me_s)
        return remote(
            count_src.at[to[0] * n_chan + to[1]], count_in.at[i],
            count_send.at[i], count_recv.at[i], to,
        )

    def first_copy(h, k, o, to):
        t = (me_t + o) % n_tile
        return remote(
            partial.at[h, k, t], first.at[h, k, t],
            first_send.at[h, k, o], first_recv.at[h, k, o], (me_t, to, me_s),
        )

    def second_copy(h, o):
        t = (me_t + o) % n_tile
        return remote(
            second_src.at[h, t], second.at[h, t],
            second_send.at[h, o], second_recv.at[h, o], (me_t, far[h], me_s),
        )

    def third_copy(h, o):
        t = (me_t + o) % n_tile
        return remote(
            third_src.at[h, o], third.at[h, o],
            third_send.at[h, o], third_recv.at[h, o], (t, me_c, me_s),
        )

    turns = tuple(range(1, n_tile)) + (0,)
    for o in range(1, n_chan):
        weight_copy(o).start()
    for a in range(n_tile):
        for b in range(n_chan):
            if a or b:
                count_copy(a, b).start()

    def grid_block(step, carry):
        h, k = step % 2, step // 2
        to = near[0] * (1 - h) + near[1] * h
        away = near[1] * (1 - h) + near[0] * h
        picks = (diagonal, to, away, me_c)
        j = sum(p * (1 - jnp.minimum(jnp.abs(k - i), 1)) for i, p in enumerate(picks))
        base = (h * n_chan + j) * block
        ids = lax.broadcasted_iota(jnp.int32, (block, rows), 0)
        onehot[...] = (ids == position[...] - base).astype(bf16)
        sums = jnp.dot(onehot[...], masked[...], preferred_element_type=f32)
        for t in range(n_tile):
            partial[h, k, t] = sums[:, t * width:(t + 1) * width].astype(bf16)

        @pl.when(k < 2)
        def _():
            for o in turns:
                first_copy(h, k, o, to).start()

        return carry

    lax.fori_loop(0, 8, grid_block, 0)

    for o in turns:
        t = (me_t + o) % n_tile
        for h in range(2):
            first_copy(h, 0, o, near[h]).wait_recv()
            second_src[h, t] = (
                partial[h, 2, t].astype(f32) + first[h, 0, t].astype(f32)
            ).astype(bf16)
            second_copy(h, o).start()
    for o in range(1, n_chan):
        weight_copy(o).wait_recv()
        pass_copy(o).start()
    for o in turns:
        t = (me_t + o) % n_tile
        for h in range(2):
            first_copy(h, 1, o, near[h]).wait_recv()
            second_copy(h, o).wait_recv()
            third_src[h, o] = (
                partial[h, 3, t].astype(f32)
                + first[h, 1, t].astype(f32)
                + second[h, t].astype(f32)
            ).astype(bf16)
            if o:
                third_copy(h, o).start()

    total = count_src[me_t * n_chan + me_c]
    for a in range(n_tile):
        for b in range(n_chan):
            if a or b:
                count_copy(a, b).wait_recv()
                total = total + count_in[a * n_chan + b]
    divisor = jnp.maximum(total, 1.0)

    for h in range(2):
        for o in range(1, n_tile):
            third_copy(h, o).wait_recv()
        summed = third_src[h, 0].astype(f32)
        for o in range(1, n_tile):
            summed = summed + third[h, o].astype(f32)
        for u in range(block // 128):
            line = divisor[h * 2 + u:h * 2 + u + 1, :]
            each = jnp.transpose(jnp.broadcast_to(line, (128, 128)))
            means[h, u * 128:(u + 1) * 128] = (summed[u * 128:(u + 1) * 128] / each).astype(bf16)

    mean_src[...] = means[other]
    mean_copy = remote(mean_src, mean_in, mean_send, mean_recv, (me_t, me_c, other))
    mean_copy.start()
    for o in range(1, n_chan):
        pass_copy(o).wait_recv()
    mean_copy.wait_recv()
    mine, theirs = means[me_s], mean_in[...]
    even = me_s == 0
    slots = (jnp.where(even, mine, theirs), jnp.where(even, theirs, mine))
    lane = lax.broadcasted_iota(jnp.int32, (half_cols, 128), 1)
    for c in range(n_chan):
        taps = []
        for b in range(2):
            acc = jnp.zeros((quarter, 128), f32)
            for a in range(2):
                at_row = (2 * a + b) * quarter
                for s in range(2):
                    acc = acc + jnp.dot(
                        slots[s][at_row:at_row + quarter],
                        weights[c, a, s * width:(s + 1) * width, :],
                        preferred_element_type=f32,
                    )
            taps.append(acc)
        low = taps[0] + pltpu.roll(taps[1], 64, 1)
        high = pltpu.roll(taps[0], 64, 1) + taps[1]
        encoded = jnp.where(lane < 64, low[:half_cols], high[half_cols:])
        hidden_src[c] = jax.nn.gelu(encoded).astype(bf16)

    here = (me_t * n_core + me_s) * n_chan + me_c
    count = n_tile * n_core * n_chan

    def hidden_copy(i):
        to = at(*offsets[i])
        return remote(
            hidden_src.at[to[1]], hidden_all.at[here + 1],
            hidden_send.at[i], hidden_recv.at[i], to,
        )

    for i in range(len(offsets)):
        hidden_copy(i).start()
    hidden_all[here + 1] = hidden_src[me_c]
    hidden_all[0] = jnp.zeros((half_cols, 128), bf16)
    hidden_all[count + 1] = jnp.zeros((half_cols, 128), bf16)
    for o in range(1, n_chan):
        weight_copy(o).wait_send()
        pass_copy(o).wait_send()
    for a in range(n_tile):
        for b in range(n_chan):
            if a or b:
                count_copy(a, b).wait_send()
    for o in turns:
        for h in range(2):
            first_copy(h, 0, o, near[h]).wait_send()
            first_copy(h, 1, o, near[h]).wait_send()
            second_copy(h, o).wait_send()
            if o:
                third_copy(h, o).wait_send()
    mean_copy.wait_send()
    for i in range(len(offsets)):
        hidden_copy(i).wait_recv()
    line = lax.broadcasted_iota(jnp.int32, (half_cols, 128), 0)
    for t in range(n_tile):
        j = jnp.int32(0)
        for i in range(n_chan):
            j = jnp.where(owners_ref[t, i] == me_t, i, j)
        at_piece = (t * n_core + me_s) * n_chan + j + 1
        total = jnp.zeros((half_cols, 128), f32)
        for p in range(3):
            field = hidden_all[at_piece + p - 1].astype(f32)
            before = jnp.where(line >= 2, pltpu.roll(field, 2, 0), 0.0)
            after = jnp.where(line < half_cols - 2, pltpu.roll(field, half_cols - 2, 0), 0.0)
            for q, shifted in enumerate((before, field, after)):
                total = total + shifted * depth_ref[3 * p + q:3 * p + q + 1, :]
            if p == 1:
                middle = field
        latent = middle + total
        out_ref[t, 0:half_cols] = latent[:, :64].astype(bf16)
        out_ref[t, half_cols:] = latent[:, 64:].astype(bf16)
    for i in range(len(offsets)):
        hidden_copy(i).wait_send()


def fused(observed_values, observed_tile, observed_cell, patch_weight, depth_weight, owners):
    f32, bf16 = jnp.float32, jnp.bfloat16
    n_tile, n_chan, n_core = (lax.axis_size(a) for a in ("tile", "chan", "tm"))
    values = observed_values[0]
    rows, width = values.shape
    depth_in, lanes = patch_weight.shape[1:]
    paired = patch_weight.reshape(2, 2, depth_in, lanes)
    paired = jnp.concatenate([paired[:, 0], paired[:, 1]], axis=2)
    depth_rows = depth_weight.astype(f32)
    depth_rows = jnp.concatenate([depth_rows, depth_rows], axis=1)
    block = HS * WS // (n_core * n_chan)
    cells = block // 4
    dma, vmem = pltpu.SemaphoreType.DMA, pltpu.VMEM
    whole = pl.BlockSpec(memory_space=pltpu.VMEM)
    pieces = n_tile * n_core * n_chan
    out = pl.pallas_call(
        fused_kernel,
        out_shape=jax.ShapeDtypeStruct((n_tile, cells, lanes), bf16),
        in_specs=[whole] * 5 + [pl.BlockSpec(memory_space=pltpu.SMEM)],
        out_specs=whole,
        scratch_shapes=[
            vmem((rows, n_tile * width), bf16),
            vmem((block, rows), bf16),
            vmem((1, rows), jnp.int32),
            vmem((2, 4, n_tile, block, width), bf16),
            vmem((2, 2, n_tile, block, width), bf16),
            vmem((2, n_tile, block, width), bf16),
            vmem((2, n_tile, block, width), bf16),
            vmem((2, n_tile, block, width), bf16),
            vmem((2, n_tile, block, width), bf16),
            vmem((n_tile * n_chan, 8, 128), f32),
            vmem((n_tile * n_chan, 8, 128), f32),
            vmem((n_chan, 2, depth_in, 2 * lanes), bf16),
            vmem((block, width), bf16),
            vmem((block, width), bf16),
            vmem((2, block, width), bf16),
            vmem((n_chan, cells // 2, 128), bf16),
            vmem((pieces + 2, cells // 2, 128), bf16),
            dma((3,)), dma((3,)), dma((3,)), dma((3,)),
            dma((n_tile * n_chan,)), dma((n_tile * n_chan,)),
            dma((2, 2, n_tile)), dma((2, 2, n_tile)),
            dma((2, n_tile)), dma((2, n_tile)),
            dma((2, n_tile)), dma((2, n_tile)),
            dma, dma,
            dma((pieces - 1,)), dma((pieces - 1,)),
        ],
        compiler_params=pltpu.CompilerParams(
            collective_id=0, has_side_effects=True, vmem_limit_bytes=48 * 2**20
        ),
    )(
        values, observed_tile.reshape(1, rows), observed_cell, paired, depth_rows, owners
    )
    return out.reshape(1, 1, n_tile, cells, lanes)


def fits(mesh):
    tile, chan, tm = (mesh.shape[a] for a in ("tile", "chan", "tm"))
    return tile == 4 and chan == 4 and tm == 2


def solution(mesh):
    placed = (
        P("tm", ("tile", "chan"), None),
        P("tm", ("tile", "chan"), None),
        P("tm", ("tile", "chan")),
        P(None, None, "chan"),
        P(None, "chan"),
        P(),
    )
    return jax.shard_map(
        fused if fits(mesh) else local,
        mesh=mesh,
        in_specs=placed,
        out_specs=P("tile", "tm", None, None, "chan"),
        check_vma=False,
    )
```

```python
import functools
import jax
import jax.numpy as jnp
from jax import lax
from jax.experimental import pallas as pl
from jax.experimental.pallas import tpu as pltpu
from jax.sharding import PartitionSpec as P

V = 128
HS = 32
WS = 64


def padded(x, sides, width):
    for axis, dim in sides:
        devices, length = (lax.axis_size(axis), x.shape[dim])
        up = [(i, (i + 1) % devices) for i in range(devices - 1)]
        down = [(j, i) for i, j in up]
        last = lax.slice_in_dim(x, length - width, length, axis=dim)
        first = lax.slice_in_dim(x, 0, width, axis=dim)
        before = lax.ppermute(last, axis, up)
        after = lax.ppermute(first, axis, down)
        x = jnp.concatenate([before, x, after], axis=dim)
    return x


def pack_rows(values, destination, placed, tile_count, capacity):
    match = (destination[:, None] == lax.iota(jnp.int32, tile_count)[None, :]).astype(jnp.int32)
    earlier = jnp.cumsum(match, axis=0) - match
    position = jnp.sum(earlier * match, axis=1)
    slot_index = destination * capacity + position
    width = values.shape[1]
    sent_values = jnp.zeros((tile_count * capacity, width), jnp.bfloat16).at[slot_index].set(values)
    sent_cells = jnp.full((tile_count * capacity,), -1, jnp.int32).at[slot_index].set(placed)
    return (
        sent_values.reshape(tile_count, capacity, width),
        sent_cells.reshape(tile_count, capacity),
    )


def grid_block(arrived_values, arrived_cells, first_cell):
    cell_ids = first_cell + lax.iota(jnp.int32, 128)
    matches = cell_ids[:, None] == arrived_cells[None, :]
    totals = jnp.dot(
        matches.astype(jnp.bfloat16), arrived_values, preferred_element_type=jnp.float32
    )
    counts = jnp.sum(matches.astype(jnp.float32), axis=1)
    return (totals, counts)


def patch_rows(field, weight, row_start, row_count):
    slab = lax.dynamic_slice_in_dim(field, 2 * row_start, 2 * row_count, 0)
    depth_in = field.shape[2]
    result = jnp.zeros((row_count * (field.shape[1] // 2), weight.shape[2]), jnp.float32)
    for tap_row in range(2):
        for tap_col in range(2):
            window = slab[tap_row::2, tap_col::2, :].reshape(-1, depth_in)
            result = result + jnp.dot(
                window, weight[tap_row * 2 + tap_col], preferred_element_type=jnp.float32
            )
    return result.reshape(row_count, field.shape[1] // 2, weight.shape[2])


def local(observed_values, observed_tile, observed_cell, patch_weight, depth_weight, owners):
    tile_count = lax.axis_size("tile")
    slot_count = lax.axis_size("tm")
    values = observed_values[0]
    capacity = 2 * values.shape[0] // tile_count
    sent_values, sent_cells = pack_rows(
        values, observed_tile[0, :, 0], observed_cell[0], tile_count, capacity
    )
    arrived = (
        lax.all_to_all(sent_values, "tile", split_axis=0, concat_axis=0, tiled=True),
        lax.all_to_all(sent_cells, "tile", split_axis=0, concat_axis=0, tiled=True),
    )
    arrived_values = arrived[0].reshape(-1, V)
    arrived_cells = arrived[1].reshape(-1)
    cell_count = HS * WS
    firsts = jnp.arange(cell_count // 128, dtype=jnp.int32) * 128
    totals, counts = lax.map(
        lambda first_cell: grid_block(arrived_values, arrived_cells, first_cell), firsts
    )
    totals = totals.reshape(cell_count, V)
    counts = counts.reshape(cell_count)
    totals, counts = (
        lax.psum(totals.astype(jnp.bfloat16), "chan").astype(jnp.float32),
        lax.psum(counts.astype(jnp.bfloat16), "chan").astype(jnp.float32),
    )
    means = (totals / jnp.maximum(counts, 1.0)[:, None]).astype(jnp.bfloat16)
    means = means.reshape(HS, WS, V)
    out_rows = HS // (2 * slot_count)
    half_cols = WS // 2
    stacked = lax.all_gather(means, "tm", axis=2, tiled=True)
    encoded = patch_rows(stacked, patch_weight, lax.axis_index("tm") * out_rows, out_rows)
    hidden = jax.nn.gelu(encoded).astype(jnp.bfloat16)
    rimmed = padded(hidden, ((("tile", "tm"), 0),), 2)
    widened = jnp.pad(rimmed, ((0, 0), (2, 2), (0, 0))).astype(jnp.float32)
    depth = jnp.zeros(hidden.shape, jnp.float32)
    for tap_row in range(3):
        for tap_col in range(3):
            shifted = widened[
                2 * tap_row : 2 * tap_row + out_rows, 2 * tap_col : 2 * tap_col + half_cols, :
            ]
            depth = depth + shifted * depth_weight[tap_row * 3 + tap_col].astype(jnp.float32)
    latent = (hidden.astype(jnp.float32) + depth).astype(jnp.bfloat16)
    channels = latent.shape[2]
    pieces = latent.reshape(tile_count, -1, channels)
    own_row = lax.dynamic_index_in_dim(owners, lax.axis_index("tile"), 0, keepdims=False)
    order = lax.iota(jnp.int32, tile_count)
    chosen = jnp.sum(
        order[None, :] * (own_row[None, :] == order[:, None]).astype(jnp.int32), axis=1
    )
    outgoing = pieces[chosen]
    received = lax.all_to_all(outgoing, "tile", split_axis=0, concat_axis=0, tiled=True)
    return received.reshape(1, 1, tile_count, -1, channels)


def fused_kernel(
    values_hbm, column_hbm, tile_hbm, cell_hbm, weight_hbm, depth_hbm, owners_hbm, out_ref,
    values_ref, column_ref, tile_ref, cell_ref, depth_ref, owners_ref,
    masked, onehot, position, partial, first, second_src, second, third_src, third,
    count_src, count_in, weights, mean_src, mean_in, means, hidden_src, hidden_all,
    load_sems,
    weight_send, weight_recv, pass_send, pass_recv, count_send, count_recv,
    first_send, first_recv, second_send, second_recv, third_send, third_recv,
    mean_send, mean_recv, hidden_send, hidden_recv,
):
    f32, bf16 = jnp.float32, jnp.bfloat16
    n_tile, n_chan, n_core = (lax.axis_size(a) for a in ("tile", "chan", "tm"))
    me_t, me_c, me_s = (lax.axis_index(a) for a in ("tile", "chan", "tm"))
    rows, width = values_ref.shape
    block = partial.shape[3]
    quarter = block // 4
    half_cols = WS // 2
    flip_x = me_c + 1 - 2 * (me_c % 2)
    flip_y = (me_c + 2) % 4
    diagonal = 3 - me_c
    near = (flip_x, flip_y)
    far = (flip_y, flip_x)
    other = 1 - me_s
    last = n_tile - 1

    def remote(source, target, send, recv, device):
        return pltpu.make_async_remote_copy(
            src_ref=source, dst_ref=target, send_sem=send, recv_sem=recv,
            device_id=device, device_id_type=pl.DeviceIdType.MESH,
        )

    offsets = [
        (a, b, c) for a in range(n_tile) for b in range(n_chan) for c in range(n_core)
    ][1:]

    def at(a, b, c):
        return ((me_t + a) % n_tile, (me_c + b) % n_chan, (me_s + c) % n_core)

    loads = [
        pltpu.make_async_copy(source, target, load_sems.at[i])
        for i, (source, target) in enumerate((
            (weight_hbm, weights.at[me_c]), (column_hbm, column_ref), (cell_hbm, cell_ref),
            (values_hbm, values_ref), (tile_hbm, tile_ref), (depth_hbm, depth_ref),
            (owners_hbm, owners_ref),
        ))
    ]
    for load in loads:
        load.start()
    barrier = pltpu.get_barrier_semaphore()
    for offset in offsets:
        pl.semaphore_signal(
            barrier, inc=1, device_id=at(*offset), device_id_type=pl.DeviceIdType.MESH
        )

    def weight_copy(o):
        here = weights.at[me_c, me_s]
        return remote(
            here, here, weight_send.at[o - 1], weight_recv.at[o - 1],
            (me_t, (me_c + o) % n_chan, me_s),
        )

    def pass_copy(o):
        here = weights.at[(me_c - o + n_chan) % n_chan, me_s]
        return remote(
            here, here, pass_send.at[o - 1], pass_recv.at[o - 1], (me_t, me_c, other)
        )

    def count_copy(a, b):
        i = a * n_chan + b
        to = ((me_t + a) % n_tile, (me_c + b) % n_chan, me_s)
        return remote(
            count_src.at[to[0] * n_chan + to[1]], count_in.at[i],
            count_send.at[i], count_recv.at[i], to,
        )

    def first_copy(h, k, m, to):
        return remote(
            partial.at[h, k, m], first.at[h, k, m],
            first_send.at[h, k, m], first_recv.at[h, k, m], (me_t, to, me_s),
        )

    def second_copy(h, m):
        return remote(
            second_src.at[h, m], second.at[h, m],
            second_send.at[h, m], second_recv.at[h, m], (me_t, far[h], me_s),
        )

    def third_copy(h, m):
        return remote(
            third_src.at[h, m], third.at[h, m],
            third_send.at[h, m], third_recv.at[h, m],
            ((me_t + m + 1) % n_tile, me_c, me_s),
        )

    loads[1].wait()
    loads[2].wait()
    cell = cell_ref[...]
    row, col = cell // WS, cell % WS
    position[...] = (
        (row // 4) * block + (row % 2) * (2 * quarter) + (col % 2) * quarter
        + ((row % 4) // 2) * half_cols + col // 2
    )
    columns = jnp.transpose(column_ref[...].astype(f32))
    loads[0].wait()
    loads[3].wait()
    for i in range(rows // 128):
        tiles = jnp.broadcast_to(columns[:, i:i + 1], (128, width))
        taken = values_ref[i * 128:(i + 1) * 128, :].astype(f32)
        for m in range(n_tile):
            wanted = ((me_t + m + 1) % n_tile).astype(f32)
            masked[i * 128:(i + 1) * 128, m * width:(m + 1) * width] = jnp.where(
                tiles == wanted, taken, 0.0
            ).astype(bf16)
    pl.semaphore_wait(barrier, len(offsets))
    for o in range(1, n_chan):
        weight_copy(o).start()

    def grid_block(half, step, carry):
        h, k = step % 2, step // 2
        to = near[0] * (1 - h) + near[1] * h
        away = near[1] * (1 - h) + near[0] * h
        if half == 0:
            picks = (diagonal, to, away, me_c)
            j = sum(jnp.where(k == i, p, 0) for i, p in enumerate(picks))
            base = (h * n_chan + j) * block
            ids = lax.broadcasted_iota(jnp.int32, (block, rows), 0)
            onehot[step] = (ids == position[...] - base).astype(bf16)
        low = half * 2 * width
        sums = jnp.dot(
            onehot[step], masked[:, low:low + 2 * width], preferred_element_type=f32
        )
        for u in range(2):
            partial[h, k, 2 * half + u] = sums[:, u * width:(u + 1) * width].astype(bf16)

        @pl.when(k < 2)
        def _():
            for u in range(2):
                first_copy(h, k, 2 * half + u, to).start()

        return carry

    def do_second(half):
        for m in (2 * half, 2 * half + 1):
            for h in range(2):
                first_copy(h, 0, m, near[h]).wait_recv()
                second_src[h, m] = (
                    partial[h, 2, m].astype(f32) + first[h, 0, m].astype(f32)
                ).astype(bf16)
                second_copy(h, m).start()

    def do_third(half):
        for m in (2 * half, 2 * half + 1):
            for h in range(2):
                first_copy(h, 1, m, near[h]).wait_recv()
                second_copy(h, m).wait_recv()
                third_src[h, m] = (
                    partial[h, 3, m].astype(f32)
                    + first[h, 1, m].astype(f32)
                    + second[h, m].astype(f32)
                ).astype(bf16)
                if m != last:
                    third_copy(h, m).start()

    lax.fori_loop(0, 8, functools.partial(grid_block, 0), 0)
    do_second(0)
    lax.fori_loop(0, 8, functools.partial(grid_block, 1), 0)
    do_third(0)
    do_second(1)

    loads[4].wait()
    pos = position[...]
    inner = pos % block
    code = (tile_ref[...] * n_chan + (pos // block) % n_chan) * 8
    code = code + (pos // (block * n_chan)) * 2 + inner // 128
    code_ids = lax.broadcasted_iota(jnp.int32, (n_tile * n_chan * 8, rows), 0)
    lane_ids = lax.broadcasted_iota(jnp.int32, (128, rows), 0)
    counts = lax.dot_general(
        (code_ids == code).astype(bf16), (lane_ids == inner % 128).astype(bf16),
        (((1,), (1,)), ((), ())), preferred_element_type=f32,
    )
    count_src[...] = counts.reshape(n_tile * n_chan, 8, 128)
    for a in range(n_tile):
        for b in range(n_chan):
            if a or b:
                count_copy(a, b).start()
    for o in range(1, n_chan):
        weight_copy(o).wait_recv()
        pass_copy(o).start()
    do_third(1)

    here = (me_t * n_core + me_s) * n_chan + me_c
    count = n_tile * n_core * n_chan
    hidden_all[0] = jnp.zeros((half_cols, 128), bf16)
    hidden_all[count + 1] = jnp.zeros((half_cols, 128), bf16)
    loads[5].wait()
    loads[6].wait()
    taps9 = depth_ref[...].astype(f32)
    taps9 = jnp.concatenate([taps9, taps9], axis=1)

    total = count_src[me_t * n_chan + me_c]
    for a in range(n_tile):
        for b in range(n_chan):
            if a or b:
                count_copy(a, b).wait_recv()
                total = total + count_in[a * n_chan + b]
    divisor = jnp.maximum(total, 1.0)

    for h in range(2):
        for m in range(last):
            third_copy(h, m).wait_recv()
        summed = third_src[h, last].astype(f32)
        for m in range(last):
            summed = summed + third[h, m].astype(f32)
        for u in range(block // 128):
            line = divisor[h * 2 + u:h * 2 + u + 1, :]
            each = jnp.transpose(jnp.broadcast_to(line, (128, 128)))
            means[h, u * 128:(u + 1) * 128] = (summed[u * 128:(u + 1) * 128] / each).astype(bf16)

    mean_src[...] = means[other]
    mean_copy = remote(mean_src, mean_in, mean_send, mean_recv, (me_t, me_c, other))
    mean_copy.start()
    for o in range(1, n_chan):
        pass_copy(o).wait_recv()
    mean_copy.wait_recv()
    mine, theirs = means[me_s], mean_in[...]
    even = me_s == 0
    slots = (jnp.where(even, mine, theirs), jnp.where(even, theirs, mine))
    lane = lax.broadcasted_iota(jnp.int32, (half_cols, 128), 1)
    lanes = weights.shape[3]
    for c in range(n_chan):
        taps = []
        for b in range(2):
            acc = jnp.zeros((quarter, 2 * lanes), f32)
            for a in range(2):
                at_row = (2 * a + b) * quarter
                kernel = weights[c, a].reshape(2 * lanes, 2 * width)
                for s in range(2):
                    acc = acc + lax.dot_general(
                        slots[s][at_row:at_row + quarter],
                        kernel[:, s * width:(s + 1) * width],
                        (((1,), (1,)), ((), ())), preferred_element_type=f32,
                    )
            taps.append(acc)
        low = taps[0] + pltpu.roll(taps[1], 64, 1)
        high = pltpu.roll(taps[0], 64, 1) + taps[1]
        encoded = jnp.where(lane < 64, low[:half_cols], high[half_cols:])
        hidden_src[c] = jax.nn.gelu(encoded).astype(bf16)

    def hidden_copy(i):
        to = at(*offsets[i])
        return remote(
            hidden_src.at[to[1]], hidden_all.at[here + 1],
            hidden_send.at[i], hidden_recv.at[i], to,
        )

    def each_hidden(column, act):
        for i, (_, b, c) in enumerate(offsets):
            if c == 0:
                act(hidden_copy(i))
        for i, (_, b, c) in enumerate(offsets):
            if c:
                @pl.when(column(b) % (n_chan - 1) == 0)
                def _():
                    act(hidden_copy(i))

    each_hidden(lambda b: me_c, lambda copy: copy.start())
    hidden_all[here + 1] = hidden_src[me_c]
    for o in range(1, n_chan):
        weight_copy(o).wait_send()
        pass_copy(o).wait_send()
    for a in range(n_tile):
        for b in range(n_chan):
            if a or b:
                count_copy(a, b).wait_send()
    for m in range(n_tile):
        for h in range(2):
            first_copy(h, 0, m, near[h]).wait_send()
            first_copy(h, 1, m, near[h]).wait_send()
            second_copy(h, m).wait_send()
            if m != last:
                third_copy(h, m).wait_send()
    mean_copy.wait_send()
    each_hidden(lambda b: (me_c + n_chan - b) % n_chan, lambda copy: copy.wait_recv())
    line = lax.broadcasted_iota(jnp.int32, (half_cols, 128), 0)
    for t in range(n_tile):
        j = jnp.int32(0)
        for i in range(n_chan):
            j = jnp.where(owners_ref[t, i] == me_t, i, j)
        at_piece = (t * n_core + me_s) * n_chan + j + 1
        total = jnp.zeros((half_cols, 128), f32)
        for p in range(3):
            field = hidden_all[at_piece + p - 1].astype(f32)
            before = jnp.where(line >= 2, pltpu.roll(field, 2, 0), 0.0)
            after = jnp.where(line < half_cols - 2, pltpu.roll(field, half_cols - 2, 0), 0.0)
            for q, shifted in enumerate((before, field, after)):
                total = total + shifted * taps9[3 * p + q:3 * p + q + 1, :]
            if p == 1:
                middle = field
        latent = middle + total
        out_ref[t, 0:half_cols] = latent[:, :64].astype(bf16)
        out_ref[t, half_cols:] = latent[:, 64:].astype(bf16)
    each_hidden(lambda b: me_c, lambda copy: copy.wait_send())


def fused(observed_values, observed_tile, observed_cell, patch_weight, depth_weight, owners):
    f32, bf16, i32 = jnp.float32, jnp.bfloat16, jnp.int32
    n_tile, n_chan, n_core = (lax.axis_size(a) for a in ("tile", "chan", "tm"))
    values = observed_values[0]
    rows, width = values.shape
    depth_in, lanes = patch_weight.shape[1:]
    turned = jnp.swapaxes(patch_weight, 1, 2).reshape(2, 2, lanes, depth_in)
    block = HS * WS // (n_core * n_chan)
    cells = block // 4
    dma, vmem = pltpu.SemaphoreType.DMA, pltpu.VMEM
    pieces = n_tile * n_core * n_chan
    out = pl.pallas_call(
        fused_kernel,
        out_shape=jax.ShapeDtypeStruct((n_tile, cells, lanes), bf16),
        in_specs=[pl.BlockSpec(memory_space=pl.ANY)] * 7,
        out_specs=pl.BlockSpec(memory_space=pltpu.VMEM),
        scratch_shapes=[
            vmem((rows, width), bf16),
            vmem((rows // 128, 128), i32),
            vmem((1, rows), i32),
            vmem((1, rows), i32),
            vmem(depth_weight.shape, bf16),
            pltpu.SMEM(owners.shape, i32),
            vmem((rows, n_tile * width), bf16),
            vmem((8, block, rows), bf16),
            vmem((1, rows), i32),
            vmem((2, 4, n_tile, block, width), bf16),
            vmem((2, 2, n_tile, block, width), bf16),
            vmem((2, n_tile, block, width), bf16),
            vmem((2, n_tile, block, width), bf16),
            vmem((2, n_tile, block, width), bf16),
            vmem((2, n_tile, block, width), bf16),
            vmem((n_tile * n_chan, 8, 128), f32),
            vmem((n_tile * n_chan, 8, 128), f32),
            vmem((n_chan, 2, 2, lanes, depth_in), bf16),
            vmem((block, width), bf16),
            vmem((block, width), bf16),
            vmem((2, block, width), bf16),
            vmem((n_chan, cells // 2, 128), bf16),
            vmem((pieces + 2, cells // 2, 128), bf16),
            dma((7,)),
            dma((3,)), dma((3,)), dma((3,)), dma((3,)),
            dma((n_tile * n_chan,)), dma((n_tile * n_chan,)),
            dma((2, 2, n_tile)), dma((2, 2, n_tile)),
            dma((2, n_tile)), dma((2, n_tile)),
            dma((2, n_tile)), dma((2, n_tile)),
            dma, dma,
            dma((pieces - 1,)), dma((pieces - 1,)),
        ],
        compiler_params=pltpu.CompilerParams(
            collective_id=0, has_side_effects=True, vmem_limit_bytes=56 * 2**20
        ),
    )(
        values, observed_tile.reshape(rows // 128, 128), observed_tile.reshape(1, rows),
        observed_cell, turned, depth_weight, owners,
    )
    return out.reshape(1, 1, n_tile, cells, lanes)


def fits(mesh):
    tile, chan, tm = (mesh.shape[a] for a in ("tile", "chan", "tm"))
    return tile == 4 and chan == 4 and tm == 2


def solution(mesh):
    placed = (
        P("tm", ("tile", "chan"), None),
        P("tm", ("tile", "chan"), None),
        P("tm", ("tile", "chan")),
        P(None, None, "chan"),
        P(None, "chan"),
        P(),
    )
    return jax.shard_map(
        fused if fits(mesh) else local,
        mesh=mesh,
        in_specs=placed,
        out_specs=P("tile", "tm", None, None, "chan"),
        check_vma=False,
    )
```

```python
import functools
import jax
import jax.numpy as jnp
from jax import lax
from jax.experimental import pallas as pl
from jax.experimental.pallas import tpu as pltpu
from jax.sharding import PartitionSpec as P

V = 128
HS = 32
WS = 64


def padded(x, sides, width):
    for axis, dim in sides:
        devices, length = (lax.axis_size(axis), x.shape[dim])
        up = [(i, (i + 1) % devices) for i in range(devices - 1)]
        down = [(j, i) for i, j in up]
        last = lax.slice_in_dim(x, length - width, length, axis=dim)
        first = lax.slice_in_dim(x, 0, width, axis=dim)
        before = lax.ppermute(last, axis, up)
        after = lax.ppermute(first, axis, down)
        x = jnp.concatenate([before, x, after], axis=dim)
    return x


def pack_rows(values, destination, placed, tile_count, capacity):
    match = (destination[:, None] == lax.iota(jnp.int32, tile_count)[None, :]).astype(jnp.int32)
    earlier = jnp.cumsum(match, axis=0) - match
    position = jnp.sum(earlier * match, axis=1)
    slot_index = destination * capacity + position
    width = values.shape[1]
    sent_values = jnp.zeros((tile_count * capacity, width), jnp.bfloat16).at[slot_index].set(values)
    sent_cells = jnp.full((tile_count * capacity,), -1, jnp.int32).at[slot_index].set(placed)
    return (
        sent_values.reshape(tile_count, capacity, width),
        sent_cells.reshape(tile_count, capacity),
    )


def grid_block(arrived_values, arrived_cells, first_cell):
    cell_ids = first_cell + lax.iota(jnp.int32, 128)
    matches = cell_ids[:, None] == arrived_cells[None, :]
    totals = jnp.dot(
        matches.astype(jnp.bfloat16), arrived_values, preferred_element_type=jnp.float32
    )
    counts = jnp.sum(matches.astype(jnp.float32), axis=1)
    return (totals, counts)


def patch_rows(field, weight, row_start, row_count):
    slab = lax.dynamic_slice_in_dim(field, 2 * row_start, 2 * row_count, 0)
    depth_in = field.shape[2]
    result = jnp.zeros((row_count * (field.shape[1] // 2), weight.shape[2]), jnp.float32)
    for tap_row in range(2):
        for tap_col in range(2):
            window = slab[tap_row::2, tap_col::2, :].reshape(-1, depth_in)
            result = result + jnp.dot(
                window, weight[tap_row * 2 + tap_col], preferred_element_type=jnp.float32
            )
    return result.reshape(row_count, field.shape[1] // 2, weight.shape[2])


def local(observed_values, observed_tile, observed_cell, patch_weight, depth_weight, owners):
    tile_count = lax.axis_size("tile")
    slot_count = lax.axis_size("tm")
    values = observed_values[0]
    capacity = 2 * values.shape[0] // tile_count
    sent_values, sent_cells = pack_rows(
        values, observed_tile[0, :, 0], observed_cell[0], tile_count, capacity
    )
    arrived = (
        lax.all_to_all(sent_values, "tile", split_axis=0, concat_axis=0, tiled=True),
        lax.all_to_all(sent_cells, "tile", split_axis=0, concat_axis=0, tiled=True),
    )
    arrived_values = arrived[0].reshape(-1, V)
    arrived_cells = arrived[1].reshape(-1)
    cell_count = HS * WS
    firsts = jnp.arange(cell_count // 128, dtype=jnp.int32) * 128
    totals, counts = lax.map(
        lambda first_cell: grid_block(arrived_values, arrived_cells, first_cell), firsts
    )
    totals = totals.reshape(cell_count, V)
    counts = counts.reshape(cell_count)
    totals, counts = (
        lax.psum(totals.astype(jnp.bfloat16), "chan").astype(jnp.float32),
        lax.psum(counts.astype(jnp.bfloat16), "chan").astype(jnp.float32),
    )
    means = (totals / jnp.maximum(counts, 1.0)[:, None]).astype(jnp.bfloat16)
    means = means.reshape(HS, WS, V)
    out_rows = HS // (2 * slot_count)
    half_cols = WS // 2
    stacked = lax.all_gather(means, "tm", axis=2, tiled=True)
    encoded = patch_rows(stacked, patch_weight, lax.axis_index("tm") * out_rows, out_rows)
    hidden = jax.nn.gelu(encoded).astype(jnp.bfloat16)
    rimmed = padded(hidden, ((("tile", "tm"), 0),), 2)
    widened = jnp.pad(rimmed, ((0, 0), (2, 2), (0, 0))).astype(jnp.float32)
    depth = jnp.zeros(hidden.shape, jnp.float32)
    for tap_row in range(3):
        for tap_col in range(3):
            shifted = widened[
                2 * tap_row : 2 * tap_row + out_rows, 2 * tap_col : 2 * tap_col + half_cols, :
            ]
            depth = depth + shifted * depth_weight[tap_row * 3 + tap_col].astype(jnp.float32)
    latent = (hidden.astype(jnp.float32) + depth).astype(jnp.bfloat16)
    channels = latent.shape[2]
    pieces = latent.reshape(tile_count, -1, channels)
    own_row = lax.dynamic_index_in_dim(owners, lax.axis_index("tile"), 0, keepdims=False)
    order = lax.iota(jnp.int32, tile_count)
    chosen = jnp.sum(
        order[None, :] * (own_row[None, :] == order[:, None]).astype(jnp.int32), axis=1
    )
    outgoing = pieces[chosen]
    received = lax.all_to_all(outgoing, "tile", split_axis=0, concat_axis=0, tiled=True)
    return received.reshape(1, 1, tile_count, -1, channels)


def fused_kernel(
    values_hbm, column_hbm, tile_hbm, cell_hbm, weight_hbm, depth_hbm, owners_hbm, out_ref,
    values_ref, column_ref, tile_ref, cell_ref, depth_ref, owners_ref,
    masked, onehot, position, partial, first, second_src, second, third_src, third,
    count_src, count_in, weights, mean_src, mean_in, means, hidden_src, hidden_all,
    load_sems,
    weight_send, weight_recv, pass_send, pass_recv, count_send, count_recv,
    first_send, first_recv, second_send, second_recv, third_send, third_recv,
    mean_send, mean_recv, hidden_send, hidden_recv,
):
    f32, bf16 = jnp.float32, jnp.bfloat16
    n_tile, n_chan, n_core = (lax.axis_size(a) for a in ("tile", "chan", "tm"))
    me_t, me_c, me_s = (lax.axis_index(a) for a in ("tile", "chan", "tm"))
    rows, width = values_ref.shape
    block = partial.shape[3]
    quarter = block // 4
    half_cols = WS // 2
    flip_x = me_c + 1 - 2 * (me_c % 2)
    flip_y = (me_c + 2) % 4
    diagonal = 3 - me_c
    near = (flip_x, flip_y)
    far = (flip_y, flip_x)
    other = 1 - me_s
    last = n_tile - 1

    def remote(source, target, send, recv, device):
        return pltpu.make_async_remote_copy(
            src_ref=source, dst_ref=target, send_sem=send, recv_sem=recv,
            device_id=device, device_id_type=pl.DeviceIdType.MESH,
        )

    offsets = [
        (a, b, c) for a in range(n_tile) for b in range(n_chan) for c in range(n_core)
    ][1:]

    def at(a, b, c):
        return ((me_t + a) % n_tile, (me_c + b) % n_chan, (me_s + c) % n_core)

    loads = [
        pltpu.make_async_copy(source, target, load_sems.at[i])
        for i, (source, target) in enumerate((
            (weight_hbm, weights.at[me_c]), (column_hbm, column_ref), (cell_hbm, cell_ref),
            (values_hbm, values_ref), (tile_hbm, tile_ref), (depth_hbm, depth_ref),
            (owners_hbm, owners_ref),
        ))
    ]
    for load in loads:
        load.start()
    barrier = pltpu.get_barrier_semaphore()
    for offset in offsets:
        pl.semaphore_signal(
            barrier, inc=1, device_id=at(*offset), device_id_type=pl.DeviceIdType.MESH
        )

    def weight_copy(o):
        here = weights.at[me_c, me_s]
        return remote(
            here, here, weight_send.at[o - 1], weight_recv.at[o - 1],
            (me_t, (me_c + o) % n_chan, me_s),
        )

    def pass_copy(o):
        here = weights.at[(me_c - o + n_chan) % n_chan, me_s]
        return remote(
            here, here, pass_send.at[o - 1], pass_recv.at[o - 1], (me_t, me_c, other)
        )

    def count_copy(a, b):
        i = a * n_chan + b
        to = ((me_t + a) % n_tile, (me_c + b) % n_chan, me_s)
        return remote(
            count_src.at[to[0] * n_chan + to[1]], count_in.at[i],
            count_send.at[i], count_recv.at[i], to,
        )

    def first_copy(h, k, m, to):
        return remote(
            partial.at[h, k, m], first.at[h, k, m],
            first_send.at[h, k, m], first_recv.at[h, k, m], (me_t, to, me_s),
        )

    def second_copy(h, m):
        return remote(
            second_src.at[h, m], second.at[h, m],
            second_send.at[h, m], second_recv.at[h, m], (me_t, far[h], me_s),
        )

    def third_copy(h, m):
        return remote(
            third_src.at[h, m], third.at[h, m],
            third_send.at[h, m], third_recv.at[h, m],
            ((me_t + m + 1) % n_tile, me_c, me_s),
        )

    loads[1].wait()
    loads[2].wait()
    cell = cell_ref[...]
    row, col = cell // WS, cell % WS
    position[...] = (
        (row // 4) * block + (row % 2) * (2 * quarter) + (col % 2) * quarter
        + ((row % 4) // 2) * half_cols + col // 2
    )
    columns = jnp.transpose(column_ref[...].astype(f32))
    loads[0].wait()
    loads[3].wait()
    for i in range(rows // 128):
        tiles = jnp.broadcast_to(columns[:, i:i + 1], (128, width))
        taken = values_ref[i * 128:(i + 1) * 128, :].astype(f32)
        for m in range(n_tile):
            wanted = ((me_t + m + 1) % n_tile).astype(f32)
            masked[i * 128:(i + 1) * 128, m * width:(m + 1) * width] = jnp.where(
                tiles == wanted, taken, 0.0
            ).astype(bf16)
    ids = lax.broadcasted_iota(jnp.int32, (block, rows), 0)

    def grid_block(k, carry):
        for h in range(2):
            picks = (diagonal, near[h], far[h], me_c)
            j = sum(jnp.where(k == i, p, 0) for i, p in enumerate(picks))
            base = (h * n_chan + j) * block
            onehot[h * block:(h + 1) * block] = (ids == position[...] - base).astype(bf16)
        sums = jnp.dot(onehot[...], masked[...], preferred_element_type=f32)
        for h in range(2):
            for m in range(n_tile):
                partial[h, k, m] = sums[
                    h * block:(h + 1) * block, m * width:(m + 1) * width
                ].astype(bf16)
        return carry

    def do_first(half):
        for k in range(2):
            for m in (2 * half, 2 * half + 1):
                for h in range(2):
                    first_copy(h, k, m, near[h]).start()

    def do_second(half):
        for m in (2 * half, 2 * half + 1):
            for h in range(2):
                first_copy(h, 0, m, near[h]).wait_recv()
                second_src[h, m] = (
                    partial[h, 2, m].astype(f32) + first[h, 0, m].astype(f32)
                ).astype(bf16)
                second_copy(h, m).start()

    def do_third(half):
        for m in (2 * half, 2 * half + 1):
            for h in range(2):
                first_copy(h, 1, m, near[h]).wait_recv()
                second_copy(h, m).wait_recv()
                third_src[h, m] = (
                    partial[h, 3, m].astype(f32)
                    + first[h, 1, m].astype(f32)
                    + second[h, m].astype(f32)
                ).astype(bf16)
                if m != last:
                    third_copy(h, m).start()

    lax.fori_loop(0, 2, grid_block, 0)
    pl.semaphore_wait(barrier, len(offsets))
    do_first(0)
    lax.fori_loop(2, 3, grid_block, 0)
    do_second(0)
    do_first(1)
    lax.fori_loop(3, 4, grid_block, 0)
    do_third(0)
    do_second(1)
    for o in range(1, n_chan):
        weight_copy(o).start()
    loads[4].wait()
    pos = position[...]
    inner = pos % block
    code = (tile_ref[...] * n_chan + (pos // block) % n_chan) * 8
    code = code + (pos // (block * n_chan)) * 2 + inner // 128
    code_ids = lax.broadcasted_iota(jnp.int32, (n_tile * n_chan * 8, rows), 0)
    lane_ids = lax.broadcasted_iota(jnp.int32, (128, rows), 0)
    counts = lax.dot_general(
        (code_ids == code).astype(bf16), (lane_ids == inner % 128).astype(bf16),
        (((1,), (1,)), ((), ())), preferred_element_type=f32,
    )
    count_src[...] = counts.reshape(n_tile * n_chan, 8, 128)
    for a in range(n_tile):
        for b in range(n_chan):
            if a or b:
                count_copy(a, b).start()
    do_third(1)

    here = (me_t * n_core + me_s) * n_chan + me_c
    count = n_tile * n_core * n_chan
    hidden_all[0] = jnp.zeros((half_cols, 128), bf16)
    hidden_all[count + 1] = jnp.zeros((half_cols, 128), bf16)
    loads[5].wait()
    loads[6].wait()
    taps9 = depth_ref[...].astype(f32)
    taps9 = jnp.concatenate([taps9, taps9], axis=1)

    total = count_src[me_t * n_chan + me_c]
    for a in range(n_tile):
        for b in range(n_chan):
            if a or b:
                count_copy(a, b).wait_recv()
                total = total + count_in[a * n_chan + b]
    divisor = jnp.maximum(total, 1.0)

    for o in range(1, n_chan):
        weight_copy(o).wait_recv()
        pass_copy(o).start()
    for h in range(2):
        for m in range(last):
            third_copy(h, m).wait_recv()
        summed = third_src[h, last].astype(f32)
        for m in range(last):
            summed = summed + third[h, m].astype(f32)
        for u in range(block // 128):
            line = divisor[h * 2 + u:h * 2 + u + 1, :]
            each = jnp.transpose(jnp.broadcast_to(line, (128, 128)))
            means[h, u * 128:(u + 1) * 128] = (summed[u * 128:(u + 1) * 128] / each).astype(bf16)

    mean_src[...] = means[other]
    mean_copy = remote(mean_src, mean_in, mean_send, mean_recv, (me_t, me_c, other))
    mean_copy.start()
    for o in range(1, n_chan):
        pass_copy(o).wait_recv()
    mean_copy.wait_recv()
    mine, theirs = means[me_s], mean_in[...]
    even = me_s == 0
    slots = (jnp.where(even, mine, theirs), jnp.where(even, theirs, mine))
    lane = lax.broadcasted_iota(jnp.int32, (half_cols, 128), 1)
    lanes = weights.shape[3]
    for c in range(n_chan):
        taps = []
        for b in range(2):
            acc = jnp.zeros((quarter, 2 * lanes), f32)
            for a in range(2):
                at_row = (2 * a + b) * quarter
                kernel = weights[c, a].reshape(2 * lanes, 2 * width)
                for s in range(2):
                    acc = acc + lax.dot_general(
                        slots[s][at_row:at_row + quarter],
                        kernel[:, s * width:(s + 1) * width],
                        (((1,), (1,)), ((), ())), preferred_element_type=f32,
                    )
            taps.append(acc)
        low = taps[0] + pltpu.roll(taps[1], 64, 1)
        high = pltpu.roll(taps[0], 64, 1) + taps[1]
        encoded = jnp.where(lane < 64, low[:half_cols], high[half_cols:])
        hidden_src[c] = jax.nn.gelu(encoded).astype(bf16)

    def hidden_copy(i):
        to = at(*offsets[i])
        return remote(
            hidden_src.at[to[1]], hidden_all.at[here + 1],
            hidden_send.at[i], hidden_recv.at[i], to,
        )

    def each_hidden(column, act):
        for i, (_, b, c) in enumerate(offsets):
            if c == 0:
                act(hidden_copy(i))
            else:
                @pl.when(column(b) % (n_chan - 1) == 0)
                def _():
                    act(hidden_copy(i))

    each_hidden(lambda b: me_c, lambda copy: copy.start())
    hidden_all[here + 1] = hidden_src[me_c]
    for o in range(1, n_chan):
        weight_copy(o).wait_send()
        pass_copy(o).wait_send()
    for a in range(n_tile):
        for b in range(n_chan):
            if a or b:
                count_copy(a, b).wait_send()
    for m in range(n_tile):
        for h in range(2):
            first_copy(h, 0, m, near[h]).wait_send()
            first_copy(h, 1, m, near[h]).wait_send()
            second_copy(h, m).wait_send()
            if m != last:
                third_copy(h, m).wait_send()
    mean_copy.wait_send()
    each_hidden(lambda b: (me_c + n_chan - b) % n_chan, lambda copy: copy.wait_recv())
    line = lax.broadcasted_iota(jnp.int32, (half_cols, 128), 0)
    for t in range(n_tile):
        j = jnp.int32(0)
        for i in range(n_chan):
            j = jnp.where(owners_ref[t, i] == me_t, i, j)
        at_piece = (t * n_core + me_s) * n_chan + j + 1
        total = jnp.zeros((half_cols, 128), f32)
        for p in range(3):
            field = hidden_all[at_piece + p - 1].astype(f32)
            before = jnp.where(line >= 2, pltpu.roll(field, 2, 0), 0.0)
            after = jnp.where(line < half_cols - 2, pltpu.roll(field, half_cols - 2, 0), 0.0)
            for q, shifted in enumerate((before, field, after)):
                total = total + shifted * taps9[3 * p + q:3 * p + q + 1, :]
            if p == 1:
                middle = field
        latent = middle + total
        out_ref[t, 0:half_cols] = latent[:, :64].astype(bf16)
        out_ref[t, half_cols:] = latent[:, 64:].astype(bf16)
    each_hidden(lambda b: me_c, lambda copy: copy.wait_send())


def fused(observed_values, observed_tile, observed_cell, patch_weight, depth_weight, owners):
    f32, bf16, i32 = jnp.float32, jnp.bfloat16, jnp.int32
    n_tile, n_chan, n_core = (lax.axis_size(a) for a in ("tile", "chan", "tm"))
    values = observed_values[0]
    rows, width = values.shape
    depth_in, lanes = patch_weight.shape[1:]
    turned = jnp.swapaxes(patch_weight, 1, 2).reshape(2, 2, lanes, depth_in)
    block = HS * WS // (n_core * n_chan)
    cells = block // 4
    dma, vmem = pltpu.SemaphoreType.DMA, pltpu.VMEM
    pieces = n_tile * n_core * n_chan
    out = pl.pallas_call(
        fused_kernel,
        out_shape=jax.ShapeDtypeStruct((n_tile, cells, lanes), bf16),
        in_specs=[pl.BlockSpec(memory_space=pl.ANY)] * 7,
        out_specs=pl.BlockSpec(memory_space=pltpu.VMEM),
        scratch_shapes=[
            vmem((rows, width), bf16),
            vmem((rows // 128, 128), i32),
            vmem((1, rows), i32),
            vmem((1, rows), i32),
            vmem(depth_weight.shape, bf16),
            pltpu.SMEM(owners.shape, i32),
            vmem((rows, n_tile * width), bf16),
            vmem((2 * block, rows), bf16),
            vmem((1, rows), i32),
            vmem((2, 4, n_tile, block, width), bf16),
            vmem((2, 2, n_tile, block, width), bf16),
            vmem((2, n_tile, block, width), bf16),
            vmem((2, n_tile, block, width), bf16),
            vmem((2, n_tile, block, width), bf16),
            vmem((2, n_tile, block, width), bf16),
            vmem((n_tile * n_chan, 8, 128), f32),
            vmem((n_tile * n_chan, 8, 128), f32),
            vmem((n_chan, 2, 2, lanes, depth_in), bf16),
            vmem((block, width), bf16),
            vmem((block, width), bf16),
            vmem((2, block, width), bf16),
            vmem((n_chan, cells // 2, 128), bf16),
            vmem((pieces + 2, cells // 2, 128), bf16),
            dma((7,)),
            dma((3,)), dma((3,)), dma((3,)), dma((3,)),
            dma((n_tile * n_chan,)), dma((n_tile * n_chan,)),
            dma((2, 2, n_tile)), dma((2, 2, n_tile)),
            dma((2, n_tile)), dma((2, n_tile)),
            dma((2, n_tile)), dma((2, n_tile)),
            dma, dma,
            dma((pieces - 1,)), dma((pieces - 1,)),
        ],
        compiler_params=pltpu.CompilerParams(
            collective_id=0, has_side_effects=True, vmem_limit_bytes=56 * 2**20
        ),
    )(
        values, observed_tile.reshape(rows // 128, 128), observed_tile.reshape(1, rows),
        observed_cell, turned, depth_weight, owners,
    )
    return out.reshape(1, 1, n_tile, cells, lanes)


def fits(mesh):
    tile, chan, tm = (mesh.shape[a] for a in ("tile", "chan", "tm"))
    return tile == 4 and chan == 4 and tm == 2


def solution(mesh):
    placed = (
        P("tm", ("tile", "chan"), None),
        P("tm", ("tile", "chan"), None),
        P("tm", ("tile", "chan")),
        P(None, None, "chan"),
        P(None, "chan"),
        P(),
    )
    return jax.shard_map(
        fused if fits(mesh) else local,
        mesh=mesh,
        in_specs=placed,
        out_specs=P("tile", "tm", None, None, "chan"),
        check_vma=False,
    )
```
